512 devices in a mesh: ctx: 16 (over z), exp: 32 (over y, x, core).
Axes of the slice: x: 4, y: 4, z: 16, core: 2. Of those that a mesh axis runs over, the one named last changes fastest.
Arguments:
- tokens: bfloat16 [65536, 2048], P(('ctx', 'exp')), may hold values from -6 to 6
- expert_ids: int32 [65536, 1], P(('ctx', 'exp')), may hold values from 0 to 31; in each aligned block of 128 rows (0 to 127, 128 to 255, ...) at most 5 rows name the same one
- gate_weights: float32 [65536, 1], P(('ctx', 'exp')), may hold values from 0.1 to 1
- weight_gate: bfloat16 [32, 2048, 1024], P('exp', 'ctx'), may hold values from -0.125 to 0.125
- weight_up: bfloat16 [32, 2048, 1024], P('exp', 'ctx'), may hold values from -0.125 to 0.125
- weight_down: bfloat16 [32, 1024, 2048], P('exp', None, 'ctx'), may hold values from -0.1875 to 0.1875
- attn_queries: bfloat16 [65536, 2048], P(('ctx', 'exp')), may hold values from -6 to 6
- attn_keys: bfloat16 [65536, 2048], P(('ctx', 'exp')), may hold values from -6 to 6
- grad_out: bfloat16 [65536, 2048], P('ctx', 'exp'), may hold values from -6 to 6
Outputs:
- grad_tokens: bfloat16 [65536, 2048], P(('ctx', 'exp'))
- grad_queries: bfloat16 [65536, 2048], P(('ctx', 'exp'))
- grad_keys: bfloat16 [65536, 2048], P(('ctx', 'exp'))
The draws below stay inside these ranges and needn't reach their ends.
Inputs may be any that keep to these rules, and one draw needn't show every extreme that they name: `expert_ids`: each row names one expert. Within each aligned block of 128 rows (the rows of one device), no expert is named more than 5 times, a bound that some block reaches.
All inputs are finite; a program needn't handle non-finite values.
Results may differ from the reference program's by a relative error of at most 0.0085.
Values may be sent and summed in bfloat16 or wider, within the bound.
A program may use at most 64 MiB of HBM per device.

```python
import math
import jax
import jax.numpy as jnp
import numpy as np
from jax import lax

D = 2048
H = 1024
HEAD_DIM = 128
TOPK = 1
BLOCK = 512
TOK_DEV = 128
EXPERTS = 32
CAP = 5
TOKENS = 65536
N_CTX = 16
N_EXP = 32


def levels(stream_key, dims, pieces, least, top_value):
    factor_of, own = 1.0, jax.random.fold_in(stream_key, 6)
    for position, blocks in pieces:
        draws = jnp.exp(jax.random.uniform(jax.random.fold_in(own, position), (blocks,), jnp.float32, least / len(pieces), top_value / len(pieces)))
        factor_of = factor_of * jnp.repeat(draws, dims[position] // blocks).reshape([-1 if axis == position else 1 for axis in range(len(dims))])
    return factor_of


def deal_out(own_key, own, number, rows, amount, top, most, lean):
    order = jax.random.permutation(own_key, amount)
    heavy_load, usual = shares(amount, rows * top, most, lean, True), shares(amount, rows * top, most, lean, False)
    places = jnp.arange(amount)

    def named(tallies, rotation):
        used = int((tallies > 0).sum())
        fixed = max(1, used // 4)
        shifted = fixed + (places - fixed + rotation * (used - fixed)) % max(1, amount - fixed)
        return jnp.zeros((amount,), jnp.int32).at[order[jnp.where(places < fixed, places, shifted)]].set(jnp.asarray(tallies, jnp.int32))

    tallies = jnp.where(number % 4 == 0, named(heavy_load, number // 4), named(usual, number - number // 4 - 1))
    mixed = jax.random.permutation(jax.random.fold_in(own, 3), amount)
    giver, receiver = mixed[0:amount // 2 * 2:2], mixed[1:amount // 2 * 2:2]
    slack = jnp.minimum(tallies[giver] - 1, most - tallies[receiver]) // 2
    slack = jnp.where((giver == order[0]) | (receiver == order[0]) | (tallies[receiver] == 0), 0, jnp.maximum(slack, 0))
    shifted = jax.random.randint(jax.random.fold_in(own, 4), (amount // 2,), 0, 1 << 20) % (slack + 1)
    tallies = tallies.at[giver].add(-shifted).at[receiver].add(shifted)
    labels = jnp.searchsorted(jnp.cumsum(tallies), jnp.arange(rows * top), side="right").astype(jnp.int32)
    grid = labels.reshape(top, rows).T
    grid = grid[jax.random.permutation(jax.random.fold_in(own, 1), rows)]
    rotation = jax.random.randint(jax.random.fold_in(own, 2), (rows, 1), 0, top)
    return jnp.take_along_axis(grid, (jnp.arange(top)[None, :] + rotation) % top, axis=1)


def shares(count, total, bound, skew, full):
    loads = [(1 << 20) // math.isqrt(grade ** skew) + 1 for grade in range(1, count + 1)]
    largest = bound if full else min(bound, max(-(-total // count), total * loads[0] // sum(loads)))
    least = 1 if total - largest >= count - 1 else 0
    counts, spare = [largest] + [least] * (count - 1), total - largest - least * (count - 1)
    while spare > 0:
        candidates = [i for i in range(1, count) if counts[i] < largest] or [i for i in range(1, count) if counts[i] < bound]
        mass, budget = sum([loads[i] for i in candidates]), spare
        for i in candidates:
            extra = min(bound - counts[i], max(1, budget * loads[i] // mass), spare)
            counts[i] = counts[i] + extra
            spare = spare - extra
    return np.array(counts)


def bell_draw(own_key, dims, spread, bound, pieces=(), kind=jnp.bfloat16):
    result = spread * jax.random.normal(own_key, dims, jnp.float32)
    if pieces:
        result = result * levels(own_key, dims, pieces, -0.22, 0.18)
    return jnp.clip(result, -bound, bound).astype(kind)


def setup_inputs(seed: int = 0) -> dict:
    streams_of = jax.random.split(jax.random.key(seed), 10)
    tokens = bell_draw(streams_of[0], (TOKENS, D), 1.0, 6.0, ((0, 512),))
    expert_ids_keys = jax.random.split(jax.random.fold_in(streams_of[1], 1), TOKENS // TOK_DEV)
    expert_ids_turns = jax.random.permutation(jax.random.fold_in(streams_of[1], 3), TOKENS // TOK_DEV)
    expert_ids = jax.vmap(lambda own, number: deal_out(jax.random.fold_in(streams_of[1], 2), own, number, TOK_DEV, EXPERTS, TOPK, CAP, 2))(expert_ids_keys, expert_ids_turns).reshape((TOKENS, TOPK))
    gate_weights = jnp.clip(jnp.exp(math.log(1.0) - 2.3025851 * jax.random.uniform(streams_of[2], (TOKENS, TOPK), jnp.float32) ** levels(streams_of[2], (TOKENS, TOPK), ((0, 512),), -0.2, 0.2)), 0.1, 1.0)
    weight_gate = bell_draw(streams_of[3], (EXPERTS, D, H), D ** -0.5, 0.125, ((0, 32), (1, 16)))
    weight_up = bell_draw(streams_of[4], (EXPERTS, D, H), D ** -0.5, 0.125, ((0, 32), (1, 16)))
    weight_down = bell_draw(streams_of[5], (EXPERTS, H, D), H ** -0.5, 0.1875, ((0, 32), (2, 16)))
    attn_queries = bell_draw(streams_of[6], (TOKENS, D), 1.0, 6.0, ((0, 512),))
    attn_keys = bell_draw(streams_of[7], (TOKENS, D), 1.0, 6.0, ((0, 512),))
    grad_out = bell_draw(streams_of[8], (TOKENS, D), 1.0, 6.0, ((0, 16), (1, 32)))
    return {"tokens": tokens, "expert_ids": expert_ids, "gate_weights": gate_weights, "weight_gate": weight_gate, "weight_up": weight_up, "weight_down": weight_down, "attn_queries": attn_queries, "attn_keys": attn_keys, "grad_out": grad_out}


def silu_parts(gate_pre):
    sigmoid = jax.nn.sigmoid(gate_pre)
    activation = gate_pre * sigmoid
    silu_slope = sigmoid * (1.0 + gate_pre * (1.0 - sigmoid))
    return activation, silu_slope


def expert_forward(slot_rows, weight_one, weight_three, weight_two):
    gate_pre = jnp.dot(slot_rows, weight_one, preferred_element_type=jnp.float32)
    up_proj = jnp.dot(slot_rows, weight_three, preferred_element_type=jnp.float32)
    activation, silu_slope = silu_parts(gate_pre)
    hidden = (activation * up_proj).astype(jnp.bfloat16)
    return jnp.dot(hidden, weight_two, preferred_element_type=jnp.float32).astype(jnp.bfloat16)


def expert_backward(slot_rows, slot_grads, weight_one, weight_three, weight_two):
    gate_pre = jnp.dot(slot_rows, weight_one, preferred_element_type=jnp.float32)
    up_proj = jnp.dot(slot_rows, weight_three, preferred_element_type=jnp.float32)
    activation, silu_slope = silu_parts(gate_pre)
    grad_hidden = jnp.dot(slot_grads, weight_two.T, preferred_element_type=jnp.float32)
    grad_gate = (grad_hidden * up_proj * silu_slope).astype(jnp.bfloat16)
    grad_up = (grad_hidden * activation).astype(jnp.bfloat16)
    summed = jnp.dot(grad_gate, weight_one.T, preferred_element_type=jnp.float32)
    summed = summed + jnp.dot(grad_up, weight_three.T, preferred_element_type=jnp.float32)
    return summed.astype(jnp.bfloat16)


def block_grads(block_item, attn_scale):
    query_blk, key_blk, value_blk, cot_blk, state_start, state_after = block_item
    length = query_blk.shape[0]
    causal = jnp.arange(length)[:, None] >= jnp.arange(length)[None, :]
    scores = jnp.where(causal, jnp.dot(query_blk, key_blk.T, preferred_element_type=jnp.float32), 0.0).astype(jnp.bfloat16)
    probes = jnp.where(causal, jnp.dot(cot_blk, value_blk.T, preferred_element_type=jnp.float32), 0.0).astype(jnp.bfloat16)
    start_low = state_start.astype(jnp.bfloat16)
    after_low = state_after.astype(jnp.bfloat16)
    grad_query = attn_scale * (jnp.dot(probes, key_blk, preferred_element_type=jnp.float32)
                               + jnp.dot(cot_blk, start_low.T, preferred_element_type=jnp.float32))
    grad_key = attn_scale * (jnp.dot(probes.T, query_blk, preferred_element_type=jnp.float32)
                             + jnp.dot(value_blk, after_low.T, preferred_element_type=jnp.float32))
    grad_value = attn_scale * (jnp.dot(scores.T, cot_blk, preferred_element_type=jnp.float32)
                               + jnp.dot(key_blk, after_low, preferred_element_type=jnp.float32))
    return grad_query.astype(jnp.bfloat16), grad_key.astype(jnp.bfloat16), grad_value.astype(jnp.bfloat16)


def head_gradients(query_head, key_head, value_head, cot_head, attn_scale):
    total = query_head.shape[0]
    nblocks = total // BLOCK
    part_width = min(HEAD_DIM, D // N_EXP)
    query_blocks = query_head.reshape(nblocks, BLOCK, HEAD_DIM)
    key_blocks = key_head.reshape(nblocks, BLOCK, HEAD_DIM)
    sum_query = jnp.zeros((total, HEAD_DIM), jnp.float32)
    sum_key = jnp.zeros((total, HEAD_DIM), jnp.float32)
    value_parts = []
    for part_index in range(HEAD_DIM // part_width):
        low_col = part_index * part_width
        value_blocks = value_head[:, low_col:low_col + part_width].reshape(nblocks, BLOCK, part_width)
        cot_blocks = cot_head[:, low_col:low_col + part_width].reshape(nblocks, BLOCK, part_width)
        state_blocks = jnp.einsum('nbd,nbv->ndv', key_blocks.astype(jnp.float32), value_blocks.astype(jnp.float32))
        after_blocks = jnp.einsum('nbd,nbv->ndv', query_blocks.astype(jnp.float32), cot_blocks.astype(jnp.float32))
        state_start = jnp.cumsum(state_blocks, axis=0) - state_blocks
        state_after = jnp.sum(after_blocks, axis=0)[None] - jnp.cumsum(after_blocks, axis=0)

        def run_block(block_item):
            return block_grads(block_item, attn_scale)

        part_query, part_key, part_value = lax.map(
            run_block, (query_blocks, key_blocks, value_blocks, cot_blocks, state_start, state_after))
        sum_query = sum_query + part_query.reshape(total, HEAD_DIM).astype(jnp.float32)
        sum_key = sum_key + part_key.reshape(total, HEAD_DIM).astype(jnp.float32)
        value_parts.append(part_value.reshape(total, part_width))
    return sum_query.astype(jnp.bfloat16), sum_key.astype(jnp.bfloat16), jnp.concatenate(value_parts, axis=1)


def reference(tokens, expert_ids, gate_weights, weight_gate, weight_up, weight_down, attn_queries, attn_keys, grad_out):
    total = tokens.shape[0]
    model_width = tokens.shape[1]
    flat_ids = expert_ids.reshape(-1).astype(jnp.int32)
    slot_count = flat_ids.shape[0]
    cap_all = N_CTX * N_EXP * CAP
    one_hot = (flat_ids[:, None] == jnp.arange(EXPERTS, dtype=jnp.int32)[None, :]).astype(jnp.int32)
    slot_rank = jnp.sum((jnp.cumsum(one_hot, axis=0, dtype=jnp.int32) - one_hot) * one_hot, axis=1).astype(jnp.int32)
    slot_dest = (flat_ids * cap_all + slot_rank).astype(jnp.int32)
    slot_owner = (jnp.arange(slot_count, dtype=jnp.int32) // TOPK).astype(jnp.int32)
    slot_source = jnp.full((EXPERTS * cap_all,), total, jnp.int32).at[slot_dest].set(slot_owner)
    slot_gate = jnp.zeros((EXPERTS * cap_all,), jnp.float32).at[slot_dest].set(gate_weights.reshape(-1))
    slot_source = slot_source.reshape(EXPERTS, cap_all)
    slot_gate = slot_gate.reshape(EXPERTS, cap_all)
    padded = jnp.concatenate([tokens, jnp.zeros((1, model_width), jnp.bfloat16)], axis=0)

    def forward_expert(running, expert_item):
        source_ids, gate_row, weight_one, weight_three, weight_two = expert_item
        produced = expert_forward(padded[source_ids], weight_one, weight_three, weight_two)
        running = running.at[source_ids].add(gate_row[:, None] * produced.astype(jnp.float32))
        return running, None

    mixed_sum, unused = lax.scan(forward_expert, jnp.zeros((total + 1, model_width), jnp.float32),
                                 (slot_source, slot_gate, weight_gate, weight_up, weight_down))
    values = mixed_sum[:total].astype(jnp.bfloat16)

    attn_scale = 1.0 / (HEAD_DIM * TOKENS) ** 0.5

    def one_head(head_index):
        start = (head_index * HEAD_DIM).astype(jnp.int32)

        def column_slice(array):
            return lax.dynamic_slice_in_dim(array, start, HEAD_DIM, 1)

        return head_gradients(column_slice(attn_queries), column_slice(attn_keys), column_slice(values),
                              column_slice(grad_out), attn_scale)

    heads_query, heads_key, heads_value = lax.map(one_head, jnp.arange(D // HEAD_DIM, dtype=jnp.int32))

    def to_columns(stacked):
        return jnp.transpose(stacked, (1, 0, 2)).reshape(total, model_width)

    grad_queries = to_columns(heads_query)
    grad_keys = to_columns(heads_key)
    grad_values = to_columns(heads_value)
    padded_grads = jnp.concatenate([grad_values, jnp.zeros((1, model_width), jnp.bfloat16)], axis=0)

    def backward_expert(running, expert_item):
        source_ids, gate_row, weight_one, weight_three, weight_two = expert_item
        produced = expert_backward(padded[source_ids], padded_grads[source_ids], weight_one, weight_three, weight_two)
        running = running.at[source_ids].add(gate_row[:, None] * produced.astype(jnp.float32))
        return running, None

    grad_sum, unused = lax.scan(backward_expert, jnp.zeros((total + 1, model_width), jnp.float32),
                                (slot_source, slot_gate, weight_gate, weight_up, weight_down))
    grad_tokens = grad_sum[:total].astype(jnp.bfloat16)
    return grad_tokens, grad_queries, grad_keys
```

```python
import math

import jax
import jax.numpy as jnp
from jax import lax
from jax.sharding import PartitionSpec as P

HEAD_DIM = 128
BLOCK = 512
CAP = 5


def exp_move(buffer):
    return lax.all_to_all(buffer, "exp", split_axis=0, concat_axis=0, tiled=True)


def dot32(spec, left, right):
    return jnp.einsum(spec, left, right, preferred_element_type=jnp.float32)


def split3(value):
    high = lax.reduce_precision(value, 8, 7)
    rest = value - high
    middle = lax.reduce_precision(rest, 8, 7)
    low = rest - middle
    return [part.astype(jnp.bfloat16) for part in (high, middle, low)]


def shards(tokens, expert_ids, gate_weights, weight_gate, weight_up, weight_down, attn_queries, attn_keys, grad_out):
    n_exp = lax.axis_size("exp")
    n_ctx = lax.axis_size("ctx")
    rows, width = tokens.shape
    slots = n_exp * CAP
    span = rows * n_exp
    part = width // n_exp
    heads = width // HEAD_DIM
    attn_scale = 1.0 / math.sqrt(HEAD_DIM * span * n_ctx)

    full_gate = lax.all_gather(weight_gate, "ctx", axis=1, tiled=True)[0]
    full_up = lax.all_gather(weight_up, "ctx", axis=1, tiled=True)[0]
    full_down = lax.all_gather(weight_down, "ctx", axis=2, tiled=True)[0]

    ids = expert_ids[:, 0]
    chosen = ids[:, None] == jnp.arange(n_exp, dtype=jnp.int32)[None, :]
    earlier_rows = jnp.arange(rows)[:, None] > jnp.arange(rows)[None, :]
    before = dot32("ij,je->ie", earlier_rows.astype(jnp.bfloat16), chosen.astype(jnp.bfloat16))
    rank = jnp.sum(jnp.where(chosen, before, 0.0), axis=1).astype(jnp.int32)
    dest = ids * CAP + rank
    place = (jnp.arange(slots, dtype=jnp.int32)[:, None] == dest[None, :]).astype(jnp.bfloat16)

    gate_parts = jnp.concatenate(split3(gate_weights) + [jnp.zeros((rows, HEAD_DIM - 3), jnp.bfloat16)], axis=1)
    packed = jnp.concatenate([tokens, gate_parts], axis=1)
    slot_rows = dot32("st,td->sd", place, packed).astype(jnp.bfloat16)
    arrived = exp_move(slot_rows.reshape(n_exp, CAP, width + HEAD_DIM)).reshape(slots, width + HEAD_DIM)
    expert_rows = arrived[:, :width]
    slot_gate = jnp.sum(arrived[:, width : width + 3].astype(jnp.float32), axis=1, keepdims=True)

    qkm = jnp.stack(
        [attn_queries.reshape(rows, heads, HEAD_DIM), attn_keys.reshape(rows, heads, HEAD_DIM)], axis=2
    )
    marks = jnp.broadcast_to(dest.astype(jnp.bfloat16)[:, None, None, None], (rows, heads, 1, HEAD_DIM))
    qkm = jnp.concatenate([qkm, marks], axis=2).reshape(rows, heads, 3 * HEAD_DIM)
    qkm = jnp.repeat(jnp.transpose(qkm, (1, 0, 2)), n_exp // heads, axis=0)
    qkm = exp_move(qkm)
    query = qkm[:, :, :HEAD_DIM].reshape(span, HEAD_DIM)
    key = qkm[:, :, HEAD_DIM : 2 * HEAD_DIM].reshape(span, HEAD_DIM)
    dest_all = qkm[:, :, 2 * HEAD_DIM].astype(jnp.int32)
    place_all = (jnp.arange(slots, dtype=jnp.int32)[None, :, None] == dest_all[:, None, :]).astype(jnp.bfloat16)

    nblocks = span // BLOCK
    qb = query.reshape(nblocks, BLOCK, HEAD_DIM)
    kb = key.reshape(nblocks, BLOCK, HEAD_DIM)
    gb = grad_out.reshape(nblocks, BLOCK, part)
    causal = (jnp.arange(BLOCK)[:, None] >= jnp.arange(BLOCK)[None, :])[None]
    position = lax.axis_index("ctx")
    levels = jnp.arange(n_ctx, dtype=jnp.int32)

    after_blocks = dot32("nbd,nbv->ndv", qb, gb)
    after_local = jnp.sum(after_blocks, axis=0)
    every_after = lax.all_gather(after_local, "ctx")
    after_in = jnp.sum(jnp.where((levels > position)[:, None, None], every_after, 0.0), axis=0)
    after = (after_in[None] + after_local[None] - jnp.cumsum(after_blocks, axis=0)).astype(jnp.bfloat16)
    scores = jnp.where(causal, dot32("ntd,nsd->nts", qb, kb), 0.0).astype(jnp.bfloat16)
    grad_value = (attn_scale * (dot32("nts,ntv->nsv", scores, gb) + dot32("nsd,ndv->nsv", kb, after))).astype(jnp.bfloat16)
    sent = dot32("dsm,dmv->dsv", place_all, grad_value.reshape(n_exp, rows, part)).astype(jnp.bfloat16)
    sent = jnp.transpose(sent.reshape(n_exp, n_exp, CAP, part), (1, 0, 2, 3))
    slot_grads = exp_move(sent.reshape(n_exp, slots, part))
    slot_grads = jnp.transpose(slot_grads, (1, 0, 2)).reshape(slots, width)

    gate_pre = dot32("rd,dh->rh", expert_rows, full_gate)
    up_proj = dot32("rd,dh->rh", expert_rows, full_up)
    sigmoid = jax.nn.sigmoid(gate_pre)
    activation = gate_pre * sigmoid
    slope = sigmoid * (1.0 + gate_pre * (1.0 - sigmoid))
    hidden = (activation * up_proj).astype(jnp.bfloat16)
    expert_out = lax.reduce_precision(dot32("rh,hd->rd", hidden, full_down), 8, 7)
    value_rows = (slot_gate * expert_out).astype(jnp.bfloat16)
    value_rows = jnp.transpose(value_rows.reshape(slots, n_exp, part), (1, 0, 2))
    value_rows = exp_move(value_rows).reshape(n_exp, n_exp, CAP, part)
    value_rows = jnp.transpose(value_rows, (1, 0, 2, 3)).reshape(n_exp, slots, part)
    value = dot32("dsm,dsv->dmv", place_all, value_rows).astype(jnp.bfloat16).reshape(span, part)
    vb = value.reshape(nblocks, BLOCK, part)

    state_blocks = dot32("nbd,nbv->ndv", kb, vb)
    state_local = jnp.sum(state_blocks, axis=0)
    every_state = lax.all_gather(state_local, "ctx")
    state_in = jnp.sum(jnp.where((levels < position)[:, None, None], every_state, 0.0), axis=0)
    start = (state_in[None] + jnp.cumsum(state_blocks, axis=0) - state_blocks).astype(jnp.bfloat16)
    probes = jnp.where(causal, dot32("ntv,nsv->nts", gb, vb), 0.0).astype(jnp.bfloat16)
    grad_query = attn_scale * (dot32("nts,nsd->ntd", probes, kb) + dot32("ntv,ndv->ntd", gb, start))
    grad_key = attn_scale * (dot32("nts,ntd->nsd", probes, qb) + dot32("nsv,ndv->nsd", vb, after))
    both = jnp.concatenate([grad_query.astype(jnp.bfloat16), grad_key.astype(jnp.bfloat16)], axis=2)
    home = exp_move(both.reshape(n_exp, rows, 2 * HEAD_DIM)).astype(jnp.float32)
    home = jnp.sum(home.reshape(heads, n_exp // heads, rows, 2 * HEAD_DIM), axis=1).astype(jnp.bfloat16)
    home = jnp.transpose(home, (1, 0, 2))
    grad_queries = home[:, :, :HEAD_DIM].reshape(rows, width)
    grad_keys = home[:, :, HEAD_DIM:].reshape(rows, width)

    grad_hidden = dot32("rd,hd->rh", slot_grads, full_down)
    grad_gate = (grad_hidden * up_proj * slope).astype(jnp.bfloat16)
    grad_up = (grad_hidden * activation).astype(jnp.bfloat16)
    expert_grad = dot32("rh,dh->rd", grad_gate, full_gate) + dot32("rh,dh->rd", grad_up, full_up)
    expert_grad = lax.reduce_precision(expert_grad, 8, 7)
    grad_rows = (slot_gate * expert_grad).astype(jnp.bfloat16)
    grad_home = exp_move(grad_rows.reshape(n_exp, CAP, width)).reshape(slots, width)
    grad_tokens = dot32("st,sd->td", place, grad_home).astype(jnp.bfloat16)
    return grad_tokens, grad_queries, grad_keys


def solution(mesh):
    rows = P(("ctx", "exp"), None)
    in_specs = (rows, rows, rows, P("exp", "ctx", None), P("exp", "ctx", None), P("exp", None, "ctx"), rows, rows, P("ctx", "exp"))
    return jax.shard_map(shards, mesh=mesh, in_specs=in_specs, out_specs=(rows, rows, rows), check_vma=False)
```
